32 devices in a mesh: groups: 2 (over y), ctx: 16 (over z, x, core).
Axes of the slice: x: 2, y: 2, z: 4, core: 2. Of those that a mesh axis runs over, the one named last changes fastest.
Arguments:
- queries: bfloat16 [512, 6144], P(('groups', 'ctx')), parts along dimension 0, may hold values from -8 to 8
- latents: bfloat16 [4096, 576], P(('groups', 'ctx')), parts along dimension 0, may hold values from -8 to 8
- w_uk: bfloat16 [32, 128, 512], replicated, may hold values from -0.5 to 0.5
- w_uv: bfloat16 [32, 512, 128], replicated, may hold values from -1.5 to 1.5
Outputs:
- attended: bfloat16 [512, 4096], P(('groups', 'ctx')), parts along dimension 0
The draws below stay inside these ranges and needn't reach their ends.
There are 2 independent parts, one for each index of `groups`. The reference program is written for one: setup_inputs(seed, part) draws one part's arguments, and reference() takes and returns one part's arrays. A program takes and returns all parts, laid end to end along the dimension named above; an argument that names none is the same for every part. Nothing has to cross between parts.
All inputs are finite; a program needn't handle non-finite values.
Results may differ from the reference program's by a relative error of at most 0.008.
Values may be sent and summed in bfloat16 or wider, within the bound.
No kernel may reach another device: no remote copies, remote signals or barrier semaphores. Data moves between devices by JAX's collectives and lax.ppermute only.
A program may use at most 128 MiB of HBM per device.

```python
import jax
import jax.numpy as jnp
from jax import lax

HEADS = 32
NOPE = 128
ROPE = 64
RANK = 512
VDIM = 128
TOK_DEV = 128
QRY_DEV = 16
TOKENS = 2048
QUERIES = 256


def draw_queries(key, part):
    base_key = jax.random.fold_in(key, 11)
    shape = (QUERIES, HEADS, NOPE + ROPE)
    values = jnp.clip(jax.random.normal(base_key, shape, jnp.float32), -4.0, 4.0)
    return values.reshape(QUERIES, HEADS * (NOPE + ROPE)).astype(jnp.bfloat16)


def draw_latents(key, part):
    base_key = jax.random.fold_in(key, 21)
    shape = (TOKENS, RANK + ROPE)
    values = jnp.clip(jax.random.normal(base_key, shape, jnp.float32), -4.0, 4.0)
    return values.astype(jnp.bfloat16)


def normal_values(own_key, dims, width, limit, held_as=jnp.bfloat16):
    return jnp.clip(width * jax.random.normal(own_key, dims, jnp.float32), -limit, limit).astype(held_as)


def setup_inputs(seed: int = 0, part: int = 0) -> dict:
    keys = jax.random.split(jax.random.key(seed), 5)
    own_keys = jax.random.split(jax.random.fold_in(keys[4], part), 5)
    queries = draw_queries(jax.random.fold_in(jax.random.fold_in(keys[4], part), 71), part)
    latents = draw_latents(jax.random.fold_in(jax.random.fold_in(keys[4], part), 71), part)
    w_uk = normal_values(keys[2], (HEADS, NOPE, RANK), NOPE ** -0.5, 0.5)
    w_uv = normal_values(keys[3], (HEADS, RANK, VDIM), 0.25, 1.5)
    return dict(queries=queries, latents=latents, w_uk=w_uk, w_uv=w_uv)


def reference(queries, latents, w_uk, w_uv):
    shaped = queries.reshape(QUERIES, HEADS, NOPE + ROPE)
    q_nope = shaped[:, :, :NOPE]
    q_rope = shaped[:, :, NOPE:]
    q_lat = jnp.einsum('thi,hil->thl', q_nope.astype(jnp.float32), w_uk.astype(jnp.float32)).astype(jnp.bfloat16)
    key_nope = latents[:, :RANK].astype(jnp.float32)
    key_rope = latents[:, RANK:].astype(jnp.float32)
    scale = 1.0 / jnp.sqrt(jnp.float32(NOPE + ROPE))
    key_pos = jnp.arange(TOKENS, dtype=jnp.int32)
    block_rows = min(64, QUERIES)

    def one_block(start):
        lat_block = lax.dynamic_slice_in_dim(q_lat, start, block_rows, 0).astype(jnp.float32)
        rope_block = lax.dynamic_slice_in_dim(q_rope, start, block_rows, 0).astype(jnp.float32)
        score = jnp.einsum('thl,jl->thj', lat_block, key_nope) + jnp.einsum('thr,jr->thj', rope_block, key_rope)
        score = score * scale
        row_ids = start + jnp.arange(block_rows, dtype=jnp.int32)
        query_pos = row_ids // QRY_DEV * TOK_DEV + TOK_DEV - QRY_DEV + row_ids % QRY_DEV
        allowed = key_pos[None, None, :] <= query_pos[:, None, None]
        score = jnp.where(allowed, score, -jnp.inf)
        top = lax.optimization_barrier(jnp.max(score, axis=-1, keepdims=True))
        expo = jnp.exp(score - top)
        total = lax.optimization_barrier(jnp.sum(expo, axis=-1))
        weight = expo.astype(jnp.bfloat16).astype(jnp.float32)
        o_lat = (jnp.einsum('thj,jl->thl', weight, key_nope) / total[:, :, None]).astype(jnp.bfloat16)
        result = jnp.einsum('thl,hlc->thc', o_lat.astype(jnp.float32), w_uv.astype(jnp.float32))
        return result.astype(jnp.bfloat16)
    starts = jnp.arange(0, QUERIES, block_rows, dtype=jnp.int32)
    blocks = lax.map(one_block, starts)
    return blocks.reshape(QUERIES, HEADS * VDIM)
```

```python
import functools
import math

import jax
import jax.numpy as jnp
from jax import lax
from jax.experimental import pallas as pl
from jax.experimental.pallas import tpu as pltpu
from jax.sharding import PartitionSpec as P


LOG2E = math.log2(math.e)
LOWEST = -1e30
TINY = 1e-30


def split_of(size):
    cores = 2 if size % 2 == 0 else 1
    chips = size // cores
    columns = max(d for d in range(1, chips + 1) if chips % d == 0 and d**3 <= chips)
    return chips // columns, columns, cores


def latent_query_kernel(own_ref, other_ref, w_ref, q_ref):
    heads, nope, rank = w_ref.shape
    rope = own_ref.shape[1] // heads - nope
    width = nope + rope
    rows = q_ref.shape[0] // heads
    for h in range(heads):
        at = h * width
        pair = jnp.concatenate(
            [own_ref[:, at : at + width], other_ref[:, at : at + width]], axis=0
        )[:rows]
        q_lat = jnp.dot(pair[:, :nope], w_ref[h], preferred_element_type=jnp.float32)
        q_ref[h * rows : (h + 1) * rows, :rank] = q_lat.astype(q_ref.dtype)
        q_ref[h * rows : (h + 1) * rows, rank:] = pair[:, nope:]


def attend_rows(q, keys, rank, coef, state, mask):
    score = jnp.dot(q, keys, preferred_element_type=jnp.float32)
    if mask is not None:
        score = jnp.where(mask, score, -jnp.inf)
    top = jnp.max(score, axis=-1, keepdims=True)
    top = jnp.maximum(top, LOWEST if state is None else state[0])
    expo = jnp.exp2((score - top) * coef)
    total = jnp.sum(expo, axis=-1, keepdims=True)
    acc = lax.dot_general(
        expo.astype(jnp.bfloat16),
        keys[:rank],
        (((1,), (1,)), ((), ())),
        preferred_element_type=jnp.float32,
    )
    if state is not None:
        factor = jnp.exp2((state[0] - top) * coef)
        total = total + state[1] * factor
        acc = acc + state[2] * factor
    return top, total, acc


def pack_stat(top, total):
    lane = lax.broadcasted_iota(jnp.int32, (top.shape[0], 128), 1)
    return jnp.where(lane < 64, top, total)


def first_stage_kernel(n, rank, coef, block, per_head, limit_ref, q_ref, *refs):
    pieces, (stat_ref, acc_ref) = refs[:n], refs[n:]
    keys = jnp.concatenate([p[...] for p in pieces], axis=1)
    size = pieces[0].shape[1]

    def body(i, carry):
        at = pl.multiple_of(i * block, block)
        row = lax.broadcasted_iota(jnp.int32, (block, size), 0)
        key = lax.broadcasted_iota(jnp.int32, (block, size), 1)
        inner = lax.rem(row, limit_ref[2 * n])
        second = lax.rem(row, per_head) >= limit_ref[2 * n]
        masks = []
        for p in range(n):
            base = jnp.where(second, limit_ref[2 * p + 1], limit_ref[2 * p])
            masks.append(key <= base + inner)
        top, total, acc = attend_rows(
            q_ref[pl.ds(at, block), :], keys, rank, coef, None, jnp.concatenate(masks, axis=1)
        )
        stat_ref[pl.ds(at, block), :] = pack_stat(top, total)
        acc_ref[pl.ds(at, block), :] = acc
        return carry

    lax.fori_loop(0, q_ref.shape[0] // block, body, 0)


def next_stage_kernel(n, rank, coef, block, valid_ref, q_ref, *refs):
    pieces, (stat_ref, acc_ref, stat_out, acc_out) = refs[:n], refs[n:]

    @pl.when(valid_ref[0] != 0)
    def _():
        keys = jnp.concatenate([p[...] for p in pieces], axis=1)

        def body(i, carry):
            at = pl.multiple_of(i * block, block)
            stat = stat_ref[pl.ds(at, block), :]
            state = (stat[:, :1], stat[:, 64:65], acc_ref[pl.ds(at, block), :])
            top, total, acc = attend_rows(
                q_ref[pl.ds(at, block), :], keys, rank, coef, state, None
            )
            stat_out[pl.ds(at, block), :] = pack_stat(top, total)
            acc_out[pl.ds(at, block), :] = acc
            return carry

        lax.fori_loop(0, q_ref.shape[0] // block, body, 0)


def project_kernel(per_head, qrows, stat_ref, acc_ref, w_ref, *outs):
    heads, rank, vdim = w_ref.shape
    lane = lax.broadcasted_iota(jnp.int32, (per_head, 128), 1)
    packed = jnp.zeros((per_head, 128), jnp.float32)
    for h in range(heads):
        rows = slice(h * per_head, (h + 1) * per_head)
        stat = stat_ref[rows, :]
        top, total = stat[:, :1], stat[:, 64:65]
        o_lat = (acc_ref[rows, :] / jnp.maximum(total, TINY)).astype(jnp.bfloat16)
        value = jnp.dot(o_lat, w_ref[h], preferred_element_type=jnp.float32)
        packed = jnp.where(lane == h, top, packed)
        packed = jnp.where(lane == h + 64, total, packed)
        for s, out in enumerate(outs):
            out[:, h * vdim : (h + 1) * vdim] = value[s * qrows : (s + 1) * qrows]
    for s, out in enumerate(outs):
        out[:, heads * vdim :] = packed[s * qrows : (s + 1) * qrows]


def combine_kernel(heads, coef, mine_ref, theirs_ref, out_ref):
    vdim = out_ref.shape[1] // heads
    a = mine_ref[:, heads * vdim :]
    b = theirs_ref[:, heads * vdim :]
    top = jnp.maximum(a, b)
    wa = a[:, 64:128] * jnp.exp2((a - top) * coef)[:, :64]
    wb = b[:, 64:128] * jnp.exp2((b - top) * coef)[:, :64]
    inv = 1.0 / (wa + wb)
    wa, wb = wa * inv, wb * inv
    for h in range(heads):
        at = slice(h * vdim, (h + 1) * vdim)
        out_ref[:, at] = (
            wa[:, h : h + 1] * mine_ref[:, at] + wb[:, h : h + 1] * theirs_ref[:, at]
        ).astype(out_ref.dtype)


VMEM = pl.BlockSpec(memory_space=pltpu.VMEM)
SMEM = pl.BlockSpec(memory_space=pltpu.SMEM)


def params(mib):
    return pltpu.CompilerParams(vmem_limit_bytes=mib * 1024 * 1024)


def cost(flops, moved, exps=0):
    return pl.CostEstimate(flops=flops, bytes_accessed=moved, transcendentals=exps)


def body(size, queries, latents, w_uk, w_uv):
    levels, columns, cores = split_of(size)
    heads, nope, rank = w_uk.shape
    vdim = w_uv.shape[2]
    qrows, krows = queries.shape[0], latents.shape[0]
    width = latents.shape[1]
    rope = width - rank
    coef = LOG2E / math.sqrt(nope + rope)
    per_head = qrows * cores
    rows = heads * per_head
    block = math.gcd(rows, 256)

    def place(z, x, c):
        return (z * columns + x) * cores + c

    sites = [
        (z, x, c) for z in range(levels) for x in range(columns) for c in range(cores)
    ]

    def up(value, by):
        pairs = [(place(z, x, c), place(z + by, x, c)) for z, x, c in sites if z + by < levels]
        return lax.ppermute(value, "ctx", pairs)

    def across(value, by):
        pairs = [(place(z, x, c), place(z, (x + by) % columns, c)) for z, x, c in sites]
        return lax.ppermute(value, "ctx", pairs)

    def partner(value):
        pairs = [(place(z, x, c), place(z, x, (c + 1) % cores)) for z, x, c in sites]
        return lax.ppermute(value, "ctx", pairs)

    me = lax.axis_index("ctx")
    core = me % cores
    column = (me // cores) % columns
    level = me // (cores * columns)
    mate = me - core + (core + 1) % cores

    keys = latents.T
    other = partner(queries) if cores > 1 else queries
    own_level = [keys] + [across(keys, d) for d in range(1, columns)]
    lifted = [up(keys, d) for d in range(1, levels)]
    stages = [own_level] + [
        [piece] + [across(piece, d) for d in range(1, columns)] for piece in lifted
    ]

    query = pl.pallas_call(
        latent_query_kernel,
        out_shape=jax.ShapeDtypeStruct((rows, width), jnp.bfloat16),
        in_specs=[VMEM] * 3,
        out_specs=VMEM,
        compiler_params=params(16),
        cost_estimate=cost(2 * rows * nope * rank, w_uk.size * 2 + rows * width * 2),
        name="latent_query",
    )(queries, other, w_uk)

    limits = []
    for d in range(columns):
        source = (level * columns + (column - d) % columns) * cores + core
        for holder in (me, mate):
            limits.append((holder - source) * krows + krows - qrows)
    limits.append(jnp.int32(qrows))
    limit = jnp.stack(limits).astype(jnp.int32)

    state_shape = (
        jax.ShapeDtypeStruct((rows, 128), jnp.float32),
        jax.ShapeDtypeStruct((rows, rank), jnp.float32),
    )
    n_keys = columns * krows
    step_cost = cost(
        2 * rows * n_keys * (width + rank),
        rows * (width * 2 + rank * 8 + 1024) + n_keys * width * 2,
        rows * n_keys,
    )
    stat, acc = pl.pallas_call(
        functools.partial(first_stage_kernel, columns, rank, coef, block, per_head),
        out_shape=state_shape,
        in_specs=[SMEM] + [VMEM] * (columns + 1),
        out_specs=(VMEM, VMEM),
        compiler_params=params(16),
        cost_estimate=step_cost,
        name="first_stage",
    )(limit, query, *stages[0])
    for d in range(1, levels):
        valid = (level >= d).astype(jnp.int32).reshape(1)
        stat, acc = pl.pallas_call(
            functools.partial(next_stage_kernel, columns, rank, coef, block),
            out_shape=state_shape,
            in_specs=[SMEM] + [VMEM] * (columns + 3),
            out_specs=(VMEM, VMEM),
            input_output_aliases={columns + 2: 0, columns + 3: 1},
            compiler_params=params(16),
            cost_estimate=step_cost,
            name="next_stage",
        )(valid, query, *stages[d], stat, acc)

    sent = jax.ShapeDtypeStruct((qrows, heads * vdim + 128), jnp.float32)
    parts = pl.pallas_call(
        functools.partial(project_kernel, per_head, qrows),
        out_shape=(sent,) * cores,
        in_specs=[VMEM] * 3,
        out_specs=(VMEM,) * cores,
        compiler_params=params(24),
        cost_estimate=cost(2 * rows * rank * vdim, w_uv.size * 2 + rows * rank * 4),
        name="project",
    )(stat, acc, w_uv)
    if cores == 1:
        return parts[0][:, : heads * vdim].astype(jnp.bfloat16)
    return pl.pallas_call(
        functools.partial(combine_kernel, heads, coef),
        out_shape=jax.ShapeDtypeStruct((qrows, heads * vdim), jnp.bfloat16),
        in_specs=[VMEM] * 2,
        out_specs=VMEM,
        compiler_params=params(16),
        cost_estimate=cost(6 * qrows * heads * vdim, qrows * heads * vdim * 10),
        name="combine",
    )(parts[0], partner(parts[1]))


def solution(mesh):
    placed = (P(("groups", "ctx"), None), P(("groups", "ctx"), None), P(), P())
    return jax.shard_map(
        functools.partial(body, mesh.shape["ctx"]),
        mesh=mesh,
        in_specs=placed,
        out_specs=P(("groups", "ctx"), None),
        check_vma=False,
    )
```
